32 devices in a mesh: section: 2 (over core), fsdp: 8 (over z, y), tensor: 2 (over x).
Axes of the slice: x: 2, y: 2, z: 4, core: 2. Of those that a mesh axis runs over, the one named last changes fastest.
Arguments:
- inputs: bfloat16 [2, 1024, 1024], P(None, 'fsdp'), may hold values from -6 to 6
- cotangent: float32 [2, 2, 1024, 1024], P('section', None, 'fsdp'), may hold values from -8 to 8
- norm_gains: bfloat16 [2, 2, 1024], P('section', None, 'fsdp'), may hold values from 0.5 to 1.5
- norm_biases: bfloat16 [2, 2, 1024], P('section', None, 'fsdp'), may hold values from -1.796875 to 1.796875
- w_qkv: bfloat16 [2, 1024, 3, 1024], P('section', 'fsdp', None, 'tensor'), may hold values from -0.1875 to 0.1875
- w_out: bfloat16 [2, 1024, 1024], P('section', 'tensor', 'fsdp'), may hold values from -0.75 to 0.75
- w_up: bfloat16 [2, 1024, 4096], P('section', 'fsdp', 'tensor'), may hold values from -0.1875 to 0.1875
- w_down: bfloat16 [2, 4096, 1024], P('section', 'tensor', 'fsdp'), may hold values from -0.09375 to 0.09375
Outputs:
- section_out: bfloat16 [2, 2, 1024, 1024], P('section', None, 'fsdp')
- input_grads: float32 [2, 2, 1024, 1024], P('section', None, 'fsdp')
- gain_grads: float32 [2, 2, 1024], P('section', None, 'fsdp')
- bias_grads: float32 [2, 2, 1024], P('section', None, 'fsdp')
- qkv_grads: float32 [2, 1024, 3, 1024], P('section', 'fsdp', None, 'tensor')
- out_grads: float32 [2, 1024, 1024], P('section', 'tensor', 'fsdp')
- up_grads: float32 [2, 1024, 4096], P('section', 'fsdp', 'tensor')
- down_grads: float32 [2, 4096, 1024], P('section', 'tensor', 'fsdp')
The draws below stay inside these ranges and needn't reach their ends.
All inputs are finite; a program needn't handle non-finite values.
Results may differ from the reference program's by a relative error of at most 0.014.
Values may be sent and summed in bfloat16 or wider, within the bound.
A program may use at most 128 MiB of HBM per device.

```python
import math
import jax
import jax.numpy as jnp
from jax import lax

D = 1024
HEADS = 16
HD = 64
FF = 4096
MB = 2
SEQ = 128
SEQS = 8
TOKENS = 1024


def raised(drawn, stream_key, source, target, blocks, factor):
    def block_of(position):
        return (jnp.arange(drawn.shape[position]) // (drawn.shape[position] // blocks)).reshape((-1,) + (1,) * (drawn.ndim - 1 - position))

    one_side = jax.random.permutation(stream_key, blocks)[block_of(target)]
    second = (block_of(target) + blocks // 2) % blocks
    return jnp.where((block_of(source) == one_side) | (block_of(source) == second), factor * drawn, drawn)


def block_levels(own_key, shape, cuts, low, largest):
    level, own = 1.0, jax.random.fold_in(own_key, 6)
    for position, shards_of in cuts:
        heights = jnp.exp(jax.random.uniform(jax.random.fold_in(own, position), (shards_of,), jnp.float32, low / len(cuts), largest / len(cuts)))
        level = level * jnp.repeat(heights, shape[position] // shards_of).reshape([-1 if axis == position else 1 for axis in range(len(shape))])
    return level


def noise(stream_key, dims, spread, reach, cuts=(), held_as=jnp.bfloat16):
    drawn = jax.random.normal(stream_key, dims, jnp.float32) * spread
    if len(cuts) > 0:
        drawn = block_levels(stream_key, dims, cuts, -0.22, 0.18) * drawn
    return jnp.clip(drawn, min=-reach, max=reach).astype(held_as)


def gaussian_with(own_key, dims, deviation, limit, split, heavy, kind=jnp.bfloat16):
    values = deviation * jax.random.normal(own_key, dims, jnp.float32)
    if split:
        values = values * block_levels(own_key, dims, split, -0.22, 0.18)
    return jnp.clip(raised(values, jax.random.fold_in(own_key, 3), *heavy), -limit, limit).astype(kind)


def setup_inputs(seed: int = 0) -> dict:
    splits = jax.random.split(jax.random.key(seed), 9)
    return {
        "inputs": noise(splits[0], (MB, TOKENS, D), 1.0, 6.0, ((1, 8),)),
        "cotangent": gaussian_with(splits[1], (2, MB, TOKENS, D), 1.0, 8.0, ((0, 2), (2, 8)), (2, 3, 8, 2.0), jnp.float32),
        "norm_gains": jnp.clip(1.0 + 0.1 * jax.random.normal(splits[2], (2, 2, D), jnp.float32), 0.5, 1.5).astype(jnp.bfloat16),
        "norm_biases": noise(splits[3], (2, 2, D), 0.3, 1.796875, ((0, 2), (2, 8))),
        "w_qkv": noise(splits[4], (2, D, 3, D), D ** -0.5, 0.1875, ((0, 2), (1, 8), (3, 2))),
        "w_out": noise(splits[5], (2, D, D), (max(16, D * 8 // SEQ)) ** -0.5, 0.75, ((0, 2), (1, 2), (2, 8))),
        "w_up": noise(splits[6], (2, D, FF), D ** -0.5, 0.1875, ((0, 2), (1, 8), (2, 2))),
        "w_down": noise(splits[7], (2, FF, D), FF ** -0.5, 0.09375, ((0, 2), (1, 2), (2, 8))),
    }


EPS = 1e-05

def round_half(value):
    return lax.optimization_barrier(value.astype(jnp.bfloat16)).astype(jnp.float32)

def angles(positions, head_dim):
    rot = head_dim // 4
    half = rot // 2
    freq = 10000.0 ** (-(jnp.arange(half).astype(jnp.float32) * 2.0 / rot))
    theta = positions.astype(jnp.float32)[:, None] * freq[None, :]
    return (jnp.cos(theta), jnp.sin(theta))

def rotate(value, cosine, sine):
    half = cosine.shape[1]
    first = value[..., :half]
    second = value[..., half:2 * half]
    rest = value[..., 2 * half:]
    cpart = cosine[:, None, :]
    spart = sine[:, None, :]
    return jnp.concatenate([first * cpart - second * spart, second * cpart + first * spart, rest], axis=-1)

def normalize(u):
    whole = u.astype(jnp.float32)
    centred = whole - lax.optimization_barrier(jnp.mean(whole, axis=-1, keepdims=True))
    rstd = lax.rsqrt(lax.optimization_barrier(jnp.mean(centred * centred, axis=-1, keepdims=True)) + EPS)
    return (centred * rstd, rstd)

def gelu_slope(hidden):
    return 0.5 * (1.0 + lax.erf(hidden / math.sqrt(2.0))) + hidden * jnp.exp(-0.5 * hidden * hidden) / math.sqrt(2.0 * math.pi)

def masked_scores(query, key):
    scores = jnp.einsum('qhd,khd->hqk', query.astype(jnp.float32), key.astype(jnp.float32))
    places = jnp.arange(query.shape[0], dtype=jnp.int32)
    return jnp.where(places[None, :] <= places[:, None], scores, -1e+30)

def attend_one(item):
    query, key, value = item
    scores = masked_scores(query, key)
    top = lax.optimization_barrier(jnp.max(scores, axis=-1, keepdims=True))
    lse = top + jnp.log(lax.optimization_barrier(jnp.sum(jnp.exp(scores - top), axis=-1, keepdims=True)))
    probs = round_half(jnp.exp(scores - lse))
    attended = jnp.einsum('hqk,khd->qhd', probs, value.astype(jnp.float32))
    return (attended.astype(jnp.bfloat16), lse[..., 0])

def back_one(item):
    query, key, value, d_att, delta, lse = item
    scores = masked_scores(query, key)
    probs = jnp.exp(scores - lse[..., None])
    grads_f = d_att.astype(jnp.float32)
    d_probs = jnp.einsum('qhd,khd->hqk', grads_f, value.astype(jnp.float32))
    d_scores = round_half(probs * (d_probs - delta.T[..., None]))
    d_query = jnp.einsum('hqk,khd->qhd', d_scores, key.astype(jnp.float32))
    d_key = jnp.einsum('hqk,qhd->khd', d_scores, query.astype(jnp.float32))
    d_value = jnp.einsum('hqk,qhd->khd', round_half(probs), grads_f)
    return (d_query, d_key, d_value)

def by_sequence(value):
    return value.reshape((SEQS, SEQ) + value.shape[1:])

def forward(u, gains, biases, wqkv, wout, wup, wdown):
    normed, rstd = normalize(u)
    gain = gains.astype(jnp.float32)
    bias = biases.astype(jnp.float32)
    first = (normed * gain[0] + bias[0]).astype(jnp.bfloat16)
    second = (normed * gain[1] + bias[1]).astype(jnp.bfloat16)
    qkv = jnp.dot(first, wqkv.reshape(D, 3 * D), preferred_element_type=jnp.float32).reshape(TOKENS, 3, HEADS, HD)
    positions = jnp.arange(TOKENS, dtype=jnp.int32) % SEQ
    cosine, sine = angles(positions, HD)
    query = (rotate(qkv[:, 0], cosine, sine) * HD ** (-0.5)).astype(jnp.bfloat16)
    key = rotate(qkv[:, 1], cosine, sine).astype(jnp.bfloat16)
    value = qkv[:, 2].astype(jnp.bfloat16)
    pieces, lses = lax.map(attend_one, (by_sequence(query), by_sequence(key), by_sequence(value)))
    attended = pieces.reshape(TOKENS, D)
    hidden = jnp.dot(second, wup, preferred_element_type=jnp.float32)
    act = jax.nn.gelu(hidden, approximate=False).astype(jnp.bfloat16)
    total = jnp.dot(attended, wout, preferred_element_type=jnp.float32) + jnp.dot(act, wdown, preferred_element_type=jnp.float32)
    result = (u.astype(jnp.float32) + total).astype(jnp.bfloat16)
    return (result, (normed, rstd, first, second, query, key, value, attended, lses, hidden, act))

def backward(grad, saved, gains, biases, wqkv, wout, wup, wdown):
    normed, rstd, first, second, query, key, value, attended, lses, hidden, act = saved
    grad_half = grad.astype(jnp.bfloat16)
    d_down = jnp.dot(act.T, grad_half, preferred_element_type=jnp.float32)
    d_act = jnp.dot(grad_half, wdown.T, preferred_element_type=jnp.float32)
    d_hidden = (d_act * gelu_slope(hidden)).astype(jnp.bfloat16)
    d_up = jnp.dot(second.T, d_hidden, preferred_element_type=jnp.float32)
    d_second = jnp.dot(d_hidden, wup.T, preferred_element_type=jnp.float32)
    d_wout = jnp.dot(attended.T, grad_half, preferred_element_type=jnp.float32)
    d_att = jnp.dot(grad_half, wout.T, preferred_element_type=jnp.float32).astype(jnp.bfloat16).reshape(TOKENS, HEADS, HD)
    delta = lax.optimization_barrier(jnp.sum(d_att.astype(jnp.float32) * attended.reshape(TOKENS, HEADS, HD).astype(jnp.float32), axis=-1))
    d_query, d_key, d_value = lax.map(back_one, (by_sequence(query), by_sequence(key), by_sequence(value), by_sequence(d_att), by_sequence(delta), lses))
    d_query = d_query.reshape(TOKENS, HEADS, HD)
    d_key = d_key.reshape(TOKENS, HEADS, HD)
    d_value = d_value.reshape(TOKENS, HEADS, HD)
    positions = jnp.arange(TOKENS, dtype=jnp.int32) % SEQ
    cosine, sine = angles(positions, HD)
    dq_back = rotate(d_query * HD ** (-0.5), cosine, -sine)
    dk_back = rotate(d_key, cosine, -sine)
    d_qkv = jnp.stack([dq_back, dk_back, d_value], axis=1).astype(jnp.bfloat16).reshape(TOKENS, 3 * D)
    d_wqkv = jnp.dot(first.T, d_qkv, preferred_element_type=jnp.float32).reshape(D, 3, D)
    d_first = jnp.dot(d_qkv, wqkv.reshape(D, 3 * D).T, preferred_element_type=jnp.float32)
    gain = gains.astype(jnp.float32)
    d_gains = jnp.stack([lax.optimization_barrier(jnp.sum(d_first * normed, axis=0)), lax.optimization_barrier(jnp.sum(d_second * normed, axis=0))])
    d_biases = jnp.stack([lax.optimization_barrier(jnp.sum(d_first, axis=0)), lax.optimization_barrier(jnp.sum(d_second, axis=0))])
    d_norm = d_first * gain[0] + d_second * gain[1]
    d_input = grad + rstd * (d_norm - lax.optimization_barrier(jnp.mean(d_norm, axis=-1, keepdims=True)) - normed * lax.optimization_barrier(jnp.mean(d_norm * normed, axis=-1, keepdims=True)))
    return (d_input, (d_gains, d_biases, d_wqkv, d_wout, d_up, d_down))

def reference(inputs, cotangent, norm_gains, norm_biases, w_qkv, w_out, w_up, w_down):
    params = [tuple((w[s] for w in (norm_gains, norm_biases, w_qkv, w_out, w_up, w_down))) for s in range(2)]
    outs_first, outs_second, grads_first, grads_second = ([], [], [], [])
    totals = [None, None]
    for micro in range(MB):
        y_first, saved_first = forward(inputs[micro], *params[0])
        y_second, saved_second = forward(y_first, *params[1])
        d_second_in, grads_b = backward(cotangent[1, micro], saved_second, *params[1])
        d_first_in, grads_a = backward(cotangent[0, micro] + d_second_in, saved_first, *params[0])
        outs_first.append(y_first)
        outs_second.append(y_second)
        grads_first.append(d_first_in)
        grads_second.append(d_second_in)
        for s, grads in ((0, grads_a), (1, grads_b)):
            if totals[s] is None:
                totals[s] = grads
            else:
                totals[s] = tuple((a + b for a, b in zip(totals[s], grads)))
    section_out = jnp.stack([jnp.stack(outs_first), jnp.stack(outs_second)])
    input_grads = jnp.stack([jnp.stack(grads_first), jnp.stack(grads_second)])
    stacked = tuple((jnp.stack([totals[0][i], totals[1][i]]) for i in range(6)))
    return (section_out, input_grads, stacked[0], stacked[1], stacked[2], stacked[3], stacked[4], stacked[5])
```

```python
import math

import jax
import jax.numpy as jnp
from jax import lax
from jax.sharding import PartitionSpec as P

HD = 64
SEQ = 128


EPS = 1e-05


def shifted(x, axis, by):
    peers = lax.axis_size(axis)
    pairs = [(i, i + by) for i in range(peers) if 0 <= i + by < peers]
    return lax.ppermute(x, axis, pairs)


def swap_sum(x, axis):
    half = x.astype(jnp.bfloat16)
    other = lax.ppermute(half, axis, [(0, 1), (1, 0)])
    return half.astype(jnp.float32) + other.astype(jnp.float32)


def pair_sum(x, axis):
    if lax.axis_size(axis) == 2:
        return swap_sum(x, axis)
    return lax.psum(x, axis)


def turned(peers, by):
    return [(i, (i + 2 * by) % peers) for i in range(peers)]


def crossed(peers):
    return [(i, i ^ 1) for i in range(peers)]


def gather(x, axis):
    peers = lax.axis_size("fsdp")
    if peers != 8:
        return lax.all_gather(x, "fsdp", axis=axis, tiled=True)
    lines = peers // 2
    me = lax.axis_index("fsdp")
    line, side = me // 2, me % 2
    width = x.shape[axis]
    shape = x.shape[:axis] + (peers * width,) + x.shape[axis + 1 :]
    whole = jnp.zeros(shape, x.dtype)
    own = [x] + [lax.ppermute(x, "fsdp", turned(peers, by)) for by in range(1, lines)]
    for by, block in enumerate(own):
        other = lax.ppermute(block, "fsdp", crossed(peers))
        source = 2 * ((line - by) % lines)
        whole = lax.dynamic_update_slice_in_dim(whole, block, (source + side) * width, axis)
        whole = lax.dynamic_update_slice_in_dim(whole, other, (source + 1 - side) * width, axis)
    return whole


def scatter(x, axis, sent=jnp.bfloat16):
    peers = lax.axis_size("fsdp")
    if peers != 8:
        return lax.psum_scatter(
            x.astype(sent), "fsdp", scatter_dimension=axis, tiled=True
        ).astype(jnp.float32)
    lines = peers // 2
    me = lax.axis_index("fsdp")
    line, side = me // 2, me % 2
    width = x.shape[axis] // peers
    total = None
    for by in (2, 1, 3, 0):
        target = 2 * ((line + by) % lines)
        away = lax.dynamic_slice_in_dim(x, (target + 1 - side) * width, width, axis)
        mine = lax.dynamic_slice_in_dim(x, (target + side) * width, width, axis)
        part = mine + lax.ppermute(away.astype(sent), "fsdp", crossed(peers)).astype(jnp.float32)
        if by:
            part = lax.ppermute(part.astype(sent), "fsdp", turned(peers, by)).astype(jnp.float32)
        total = part if total is None else total + part
    return total


def angles(positions, head_dim):
    rot = head_dim // 4
    half = rot // 2
    freq = 10000.0 ** (-(jnp.arange(half).astype(jnp.float32) * 2.0 / rot))
    theta = positions.astype(jnp.float32)[:, None] * freq[None, :]
    return (jnp.cos(theta), jnp.sin(theta))


def rotate(value, cosine, sine):
    half = cosine.shape[1]
    first = value[..., :half]
    second = value[..., half : 2 * half]
    rest = value[..., 2 * half :]
    cpart = cosine[:, None, :]
    spart = sine[:, None, :]
    return jnp.concatenate(
        [first * cpart - second * spart, second * cpart + first * spart, rest], axis=-1
    )


def normalize(u):
    whole = u.astype(jnp.float32)
    centred = whole - jnp.mean(whole, axis=-1, keepdims=True)
    rstd = lax.rsqrt(jnp.mean(centred * centred, axis=-1, keepdims=True) + EPS)
    return (centred * rstd, rstd)


def gelu_slope(hidden):
    return 0.5 * (1.0 + lax.erf(hidden / math.sqrt(2.0))) + hidden * jnp.exp(
        -0.5 * hidden * hidden
    ) / math.sqrt(2.0 * math.pi)


def grouped(value):
    return value.reshape((value.shape[0] // SEQ, SEQ) + value.shape[1:])


def masked_scores(query, key):
    scores = jnp.einsum("sqhd,skhd->shqk", query, key, preferred_element_type=jnp.float32)
    places = jnp.arange(SEQ, dtype=jnp.int32)
    return jnp.where(places[None, :] <= places[:, None], scores, -1e30)


def attention_forward(query, key, value):
    tokens, heads = (query.shape[0], query.shape[1])
    scores = masked_scores(grouped(query), grouped(key))
    top = jnp.max(scores, axis=-1, keepdims=True)
    lse = top + jnp.log(jnp.sum(jnp.exp(scores - top), axis=-1, keepdims=True))
    probs = jnp.exp(scores - lse).astype(jnp.bfloat16)
    attended = jnp.einsum(
        "shqk,skhd->sqhd", probs, grouped(value), preferred_element_type=jnp.float32
    )
    return (attended.reshape(tokens, heads, HD), lse[..., 0])


def attention_backward(query, key, value, lse, d_att, attended):
    tokens, heads = (query.shape[0], query.shape[1])
    delta = jnp.sum(d_att.astype(jnp.float32) * attended.astype(jnp.float32), axis=-1)
    delta = jnp.swapaxes(grouped(delta), 1, 2)
    query_s, key_s, value_s, grads_s = (
        grouped(query),
        grouped(key),
        grouped(value),
        grouped(d_att),
    )
    probs = jnp.exp(masked_scores(query_s, key_s) - lse[..., None])
    d_probs = jnp.einsum("sqhd,skhd->shqk", grads_s, value_s, preferred_element_type=jnp.float32)
    d_scores = (probs * (d_probs - delta[..., None])).astype(jnp.bfloat16)
    d_query = jnp.einsum("shqk,skhd->sqhd", d_scores, key_s, preferred_element_type=jnp.float32)
    d_key = jnp.einsum("shqk,sqhd->skhd", d_scores, query_s, preferred_element_type=jnp.float32)
    d_value = jnp.einsum(
        "shqk,sqhd->skhd", probs.astype(jnp.bfloat16), grads_s, preferred_element_type=jnp.float32
    )
    shape = (tokens, heads, HD)
    return (d_query.reshape(shape), d_key.reshape(shape), d_value.reshape(shape))


def layer_forward(u, params):
    gains, biases, wqkv, wout, wup, wdown = params
    tokens, width = u.shape
    local = wqkv.shape[2]
    heads = local // HD
    normed, rstd = normalize(u)
    gain = gains.astype(jnp.float32)
    bias = biases.astype(jnp.float32)
    first = (normed * gain[0] + bias[0]).astype(jnp.bfloat16)
    second = (normed * gain[1] + bias[1]).astype(jnp.bfloat16)
    qkv = jnp.dot(
        first, wqkv.reshape(width, 3 * local), preferred_element_type=jnp.float32
    ).reshape(tokens, 3, heads, HD)
    qpos = jnp.arange(tokens, dtype=jnp.int32) % SEQ
    cosine, sine = angles(qpos, HD)
    query = (rotate(qkv[:, 0], cosine, sine) * HD ** (-0.5)).astype(jnp.bfloat16)
    key = rotate(qkv[:, 1], cosine, sine).astype(jnp.bfloat16)
    value = qkv[:, 2].astype(jnp.bfloat16)
    attended, lse = attention_forward(query, key, value)
    attended = attended.astype(jnp.bfloat16).reshape(tokens, local)
    hidden = jnp.dot(second, wup, preferred_element_type=jnp.float32)
    act = jax.nn.gelu(hidden, approximate=False).astype(jnp.bfloat16)
    branch = jnp.dot(attended, wout, preferred_element_type=jnp.float32) + jnp.dot(
        act, wdown, preferred_element_type=jnp.float32
    )
    total = pair_sum(branch, "tensor")
    result = (u.astype(jnp.float32) + total).astype(jnp.bfloat16)
    return (result, (normed, rstd, first, second, query, key, value, attended, lse, hidden, act))


def layer_backward(grad, saved, params):
    normed, rstd, first, second, query, key, value, attended, lse, hidden, act = saved
    gains, biases, wqkv, wout, wup, wdown = params
    tokens, width = grad.shape
    local = wqkv.shape[2]
    heads = local // HD
    grad_half = grad.astype(jnp.bfloat16)
    d_act = jnp.dot(grad_half, wdown.T, preferred_element_type=jnp.float32)
    d_hidden = (d_act * gelu_slope(hidden)).astype(jnp.bfloat16)
    d_second = jnp.dot(d_hidden, wup.T, preferred_element_type=jnp.float32)
    d_att = (
        jnp.dot(grad_half, wout.T, preferred_element_type=jnp.float32)
        .astype(jnp.bfloat16)
        .reshape(tokens, heads, HD)
    )
    d_query, d_key, d_value = attention_backward(
        query, key, value, lse, d_att, attended.reshape(tokens, heads, HD)
    )
    qpos = jnp.arange(tokens, dtype=jnp.int32) % SEQ
    cosine, sine = angles(qpos, HD)
    dq_back = rotate(d_query * HD ** (-0.5), cosine, -sine)
    dk_back = rotate(d_key, cosine, -sine)
    d_qkv = (
        jnp.stack([dq_back, dk_back, d_value], axis=1)
        .astype(jnp.bfloat16)
        .reshape(tokens, 3 * local)
    )
    d_first = jnp.dot(d_qkv, wqkv.reshape(width, 3 * local).T, preferred_element_type=jnp.float32)
    gain = gains.astype(jnp.float32)
    d_norms = jnp.stack(
        [
            jnp.sum(d_first * normed, axis=0),
            jnp.sum(d_second * normed, axis=0),
            jnp.sum(d_first, axis=0),
            jnp.sum(d_second, axis=0),
        ]
    )
    d_norm = pair_sum(d_first * gain[0] + d_second * gain[1], "tensor")
    d_input = grad + rstd * (
        d_norm
        - jnp.mean(d_norm, axis=-1, keepdims=True)
        - normed * jnp.mean(d_norm * normed, axis=-1, keepdims=True)
    )
    return (d_input, grad_half, d_hidden, d_qkv, d_norms)


def shards(inputs, cotangent, norm_gains, norm_biases, w_qkv, w_out, w_up, w_down):
    section = lax.axis_index("section")
    lead = section == 0
    micro = inputs.shape[0]
    width = inputs.shape[2]
    local = w_qkv.shape[3]
    norms = gather(jnp.concatenate([norm_gains[0], norm_biases[0]]), 1)
    wqkv = gather(w_qkv[0].reshape(-1, 3 * local), 0).reshape(width, 3, local)
    wup = gather(w_up[0], 0)
    wout = gather(w_out[0], 1)
    wdown = gather(w_down[0], 1)
    params = (norms[:2], norms[2:], wqkv, wout, wup, wdown)

    received = None
    runs = []
    for tick in range(micro + 1):
        own = inputs[min(tick, micro - 1)]
        entering = own if received is None else jnp.where(lead, own, received)
        result, saved = layer_forward(entering, params)
        runs.append((result,) + saved)
        if tick < micro:
            received = shifted(result, "section", 1)
    store = [
        tuple(jnp.where(lead, a, b) for a, b in zip(runs[m], runs[m + 1])) for m in range(micro)
    ]

    incoming = None
    backs = []
    for tick in range(micro + 1):
        early, late = max(tick - 1, 0), min(tick, micro - 1)
        record = store[early]
        grad = cotangent[0, early]
        if early != late:
            record = tuple(jnp.where(lead, a, b) for a, b in zip(record, store[late]))
            grad = jnp.where(lead, grad, cotangent[0, late])
        if incoming is not None:
            grad = grad + jnp.where(lead, incoming, 0.0)
        back = layer_backward(grad, record[1:], params)
        backs.append(back)
        if tick < micro:
            incoming = shifted(back[0], "section", -1)
    done = [
        tuple(jnp.where(lead, a, b) for a, b in zip(backs[m + 1], backs[m])) for m in range(micro)
    ]

    def over_tokens(left, right):
        left = jnp.concatenate([store[m][left] for m in range(micro)])
        right = jnp.concatenate([done[m][right] for m in range(micro)])
        return jnp.dot(left.T, right, preferred_element_type=jnp.float32)

    down_grads = scatter(over_tokens(11, 1), 1)
    out_grads = scatter(over_tokens(8, 1), 1)
    up_grads = scatter(over_tokens(4, 2), 0)
    qkv_grads = scatter(over_tokens(3, 3), 0).reshape(-1, 3, local)
    d_norms = sum(item[4] for item in done)
    d_norms = d_norms + lax.ppermute(d_norms, "tensor", [(0, 1), (1, 0)])
    d_norms = scatter(d_norms, 1, jnp.float32)
    return (
        jnp.stack([item[0] for item in store])[None],
        jnp.stack([item[0] for item in done])[None],
        d_norms[None, :2],
        d_norms[None, 2:],
        qkv_grads[None],
        out_grads[None],
        up_grads[None],
        down_grads[None],
    )


def solution(mesh):
    in_specs = (
        P(None, "fsdp", None),
        P("section", None, "fsdp", None),
        P("section", None, "fsdp"),
        P("section", None, "fsdp"),
        P("section", "fsdp", None, "tensor"),
        P("section", "tensor", "fsdp"),
        P("section", "fsdp", "tensor"),
        P("section", "tensor", "fsdp"),
    )
    out_specs = (
        P("section", None, "fsdp", None),
        P("section", None, "fsdp", None),
        P("section", None, "fsdp"),
        P("section", None, "fsdp"),
        P("section", "fsdp", None, "tensor"),
        P("section", "tensor", "fsdp"),
        P("section", "fsdp", "tensor"),
        P("section", "tensor", "fsdp"),
    )
    return jax.shard_map(shards, mesh=mesh, in_specs=in_specs, out_specs=out_specs, check_vma=False)
```

```python
import math

import jax
import jax.numpy as jnp
from jax import lax
from jax.sharding import PartitionSpec as P

HD = 64
SEQ = 128


EPS = 1e-05


def shifted(x, axis, by):
    peers = lax.axis_size(axis)
    pairs = [(i, i + by) for i in range(peers) if 0 <= i + by < peers]
    return lax.ppermute(x, axis, pairs)


def swap_sum(x, axis):
    half = x.astype(jnp.bfloat16)
    other = lax.ppermute(half, axis, [(0, 1), (1, 0)])
    return half.astype(jnp.float32) + other.astype(jnp.float32)


def pair_sum(x, axis):
    if lax.axis_size(axis) == 2:
        return swap_sum(x, axis)
    return lax.psum(x, axis)


def turned(peers, by):
    return [(i, (i + 2 * by) % peers) for i in range(peers)]


def crossed(peers):
    return [(i, i ^ 1) for i in range(peers)]


def gather(x, axis, after=()):
    peers = lax.axis_size("fsdp")
    if peers != 8:
        return (lax.all_gather(x, "fsdp", axis=axis, tiled=True), ())
    lines = peers // 2
    me = lax.axis_index("fsdp")
    line, side = me // 2, me % 2
    width = x.shape[axis]
    shape = x.shape[:axis] + (peers * width,) + x.shape[axis + 1 :]
    whole = jnp.zeros(shape, x.dtype)
    start = x
    if after:
        start, after = lax.optimization_barrier((x, after))
    own = [x] + [lax.ppermute(start, "fsdp", turned(peers, by)) for by in range(1, lines)]
    for by, block in enumerate(own):
        other = lax.ppermute(block, "fsdp", crossed(peers))
        source = 2 * ((line - by) % lines)
        whole = lax.dynamic_update_slice_in_dim(whole, block, (source + side) * width, axis)
        whole = lax.dynamic_update_slice_in_dim(whole, other, (source + 1 - side) * width, axis)
    return (whole, tuple(own[1:]))


TURNS = (2, 1, 3, 0)


def scatter_begin(x, axis, after=(), sent=jnp.bfloat16):
    peers = lax.axis_size("fsdp")
    if peers != 8:
        return (x, ())
    lines = peers // 2
    me = lax.axis_index("fsdp")
    line, side = me // 2, me % 2
    width = x.shape[axis] // peers

    def block(by, side):
        place = 2 * ((line + by) % lines) + side
        return lax.dynamic_slice_in_dim(x, place * width, width, axis)

    away = tuple(block(by, 1 - side).astype(sent) for by in TURNS)
    if after:
        away, after = lax.optimization_barrier((away, after))
    came = tuple(lax.ppermute(item, "fsdp", crossed(peers)) for item in away)
    return (tuple(block(by, side) for by in TURNS), came)


def scatter_end(begun, axis, sent=jnp.bfloat16):
    mine, came = begun
    peers = lax.axis_size("fsdp")
    if peers != 8:
        return lax.psum_scatter(
            mine.astype(sent), "fsdp", scatter_dimension=axis, tiled=True
        ).astype(jnp.float32)
    total = None
    for by, left, right in zip(TURNS, mine, came):
        part = left + right.astype(jnp.float32)
        if by:
            part = lax.ppermute(part.astype(sent), "fsdp", turned(peers, by)).astype(jnp.float32)
        total = part if total is None else total + part
    return total


def angles(positions, head_dim):
    rot = head_dim // 4
    half = rot // 2
    freq = 10000.0 ** (-(jnp.arange(half).astype(jnp.float32) * 2.0 / rot))
    theta = positions.astype(jnp.float32)[:, None] * freq[None, :]
    return (jnp.cos(theta), jnp.sin(theta))


def rotate(value, cosine, sine):
    half = cosine.shape[1]
    first = value[..., :half]
    second = value[..., half : 2 * half]
    rest = value[..., 2 * half :]
    cpart = cosine[:, None, :]
    spart = sine[:, None, :]
    return jnp.concatenate(
        [first * cpart - second * spart, second * cpart + first * spart, rest], axis=-1
    )


def normalize(u):
    whole = u.astype(jnp.float32)
    centred = whole - jnp.mean(whole, axis=-1, keepdims=True)
    rstd = lax.rsqrt(jnp.mean(centred * centred, axis=-1, keepdims=True) + EPS)
    return (centred * rstd, rstd)


def gelu_slope(hidden):
    return 0.5 * (1.0 + lax.erf(hidden / math.sqrt(2.0))) + hidden * jnp.exp(
        -0.5 * hidden * hidden
    ) / math.sqrt(2.0 * math.pi)


def grouped(value):
    return value.reshape((value.shape[0] // SEQ, SEQ) + value.shape[1:])


def masked_scores(query, key):
    scores = jnp.einsum("sqhd,skhd->shqk", query, key, preferred_element_type=jnp.float32)
    places = jnp.arange(SEQ, dtype=jnp.int32)
    return jnp.where(places[None, :] <= places[:, None], scores, -1e30)


def attention_forward(query, key, value):
    tokens, heads = (query.shape[0], query.shape[1])
    scores = masked_scores(grouped(query), grouped(key))
    top = jnp.max(scores, axis=-1, keepdims=True)
    lse = top + jnp.log(jnp.sum(jnp.exp(scores - top), axis=-1, keepdims=True))
    probs = jnp.exp(scores - lse).astype(jnp.bfloat16)
    attended = jnp.einsum(
        "shqk,skhd->sqhd", probs, grouped(value), preferred_element_type=jnp.float32
    )
    return (attended.reshape(tokens, heads, HD), lse[..., 0])


def attention_backward(query, key, value, lse, d_att, attended):
    tokens, heads = (query.shape[0], query.shape[1])
    delta = jnp.sum(d_att.astype(jnp.float32) * attended.astype(jnp.float32), axis=-1)
    delta = jnp.swapaxes(grouped(delta), 1, 2)
    query_s, key_s, value_s, grads_s = (
        grouped(query),
        grouped(key),
        grouped(value),
        grouped(d_att),
    )
    probs = jnp.exp(masked_scores(query_s, key_s) - lse[..., None])
    d_probs = jnp.einsum("sqhd,skhd->shqk", grads_s, value_s, preferred_element_type=jnp.float32)
    d_scores = (probs * (d_probs - delta[..., None])).astype(jnp.bfloat16)
    d_query = jnp.einsum("shqk,skhd->sqhd", d_scores, key_s, preferred_element_type=jnp.float32)
    d_key = jnp.einsum("shqk,sqhd->skhd", d_scores, query_s, preferred_element_type=jnp.float32)
    d_value = jnp.einsum(
        "shqk,sqhd->skhd", probs.astype(jnp.bfloat16), grads_s, preferred_element_type=jnp.float32
    )
    shape = (tokens, heads, HD)
    return (d_query.reshape(shape), d_key.reshape(shape), d_value.reshape(shape))


def layer_forward(u, params):
    gains, biases, wqkv, wout, wup, wdown = params
    tokens, width = u.shape
    local = wqkv.shape[2]
    heads = local // HD
    normed, rstd = normalize(u)
    gain = gains.astype(jnp.float32)
    bias = biases.astype(jnp.float32)
    first = (normed * gain[0] + bias[0]).astype(jnp.bfloat16)
    second = (normed * gain[1] + bias[1]).astype(jnp.bfloat16)
    qkv = jnp.dot(
        first, wqkv.reshape(width, 3 * local), preferred_element_type=jnp.float32
    ).reshape(tokens, 3, heads, HD)
    qpos = jnp.arange(tokens, dtype=jnp.int32) % SEQ
    cosine, sine = angles(qpos, HD)
    query = (rotate(qkv[:, 0], cosine, sine) * HD ** (-0.5)).astype(jnp.bfloat16)
    key = rotate(qkv[:, 1], cosine, sine).astype(jnp.bfloat16)
    value = qkv[:, 2].astype(jnp.bfloat16)
    attended, lse = attention_forward(query, key, value)
    attended = attended.astype(jnp.bfloat16).reshape(tokens, local)
    hidden = jnp.dot(second, wup, preferred_element_type=jnp.float32)
    act = jax.nn.gelu(hidden, approximate=False).astype(jnp.bfloat16)
    branch = jnp.dot(attended, wout, preferred_element_type=jnp.float32) + jnp.dot(
        act, wdown, preferred_element_type=jnp.float32
    )
    total = pair_sum(branch, "tensor")
    result = (u.astype(jnp.float32) + total).astype(jnp.bfloat16)
    return (result, (normed, rstd, first, second, query, key, value, attended, lse, hidden, act))


def layer_backward(grad, saved, params, held=()):
    normed, rstd, first, second, query, key, value, attended, lse, hidden, act = saved
    gains, biases, wqkv, wout, wup, wdown = params
    tokens, width = grad.shape
    local = wqkv.shape[2]
    heads = local // HD
    grad_half = grad.astype(jnp.bfloat16)
    d_act = jnp.dot(grad_half, wdown.T, preferred_element_type=jnp.float32)
    d_hidden = (d_act * gelu_slope(hidden)).astype(jnp.bfloat16)
    d_second = jnp.dot(d_hidden, wup.T, preferred_element_type=jnp.float32)
    d_att = (
        jnp.dot(grad_half, wout.T, preferred_element_type=jnp.float32)
        .astype(jnp.bfloat16)
        .reshape(tokens, heads, HD)
    )
    d_query, d_key, d_value = attention_backward(
        query, key, value, lse, d_att, attended.reshape(tokens, heads, HD)
    )
    qpos = jnp.arange(tokens, dtype=jnp.int32) % SEQ
    cosine, sine = angles(qpos, HD)
    dq_back = rotate(d_query * HD ** (-0.5), cosine, -sine)
    dk_back = rotate(d_key, cosine, -sine)
    d_qkv = (
        jnp.stack([dq_back, dk_back, d_value], axis=1)
        .astype(jnp.bfloat16)
        .reshape(tokens, 3 * local)
    )
    d_first = jnp.dot(d_qkv, wqkv.reshape(width, 3 * local).T, preferred_element_type=jnp.float32)
    gain = gains.astype(jnp.float32)
    d_norms = jnp.stack(
        [
            jnp.sum(d_first * normed, axis=0),
            jnp.sum(d_second * normed, axis=0),
            jnp.sum(d_first, axis=0),
            jnp.sum(d_second, axis=0),
        ]
    )
    d_norm = d_first * gain[0] + d_second * gain[1]
    if held:
        d_norm, held = lax.optimization_barrier((d_norm, held))
    d_norm = pair_sum(d_norm, "tensor")
    d_input = grad + rstd * (
        d_norm
        - jnp.mean(d_norm, axis=-1, keepdims=True)
        - normed * jnp.mean(d_norm * normed, axis=-1, keepdims=True)
    )
    return ((d_input, grad_half, d_hidden, d_qkv, d_norms), held)


def over_tokens(store, place, right):
    left = jnp.concatenate([item[place] for item in store])
    return jnp.dot(left.T, right, preferred_element_type=jnp.float32)


def shards(inputs, cotangent, norm_gains, norm_biases, w_qkv, w_out, w_up, w_down):
    section = lax.axis_index("section")
    lead = section == 0
    micro = inputs.shape[0]
    width = inputs.shape[2]
    local = w_qkv.shape[3]
    norms, _ = gather(jnp.concatenate([norm_gains[0], norm_biases[0]]), 1)
    wqkv, after = gather(w_qkv[0].reshape(-1, 3 * local), 0)
    wup, after = gather(w_up[0], 0, after)
    wdown, after = gather(w_down[0], 1, after)
    wout, after = gather(w_out[0], 1, after)
    wqkv = wqkv.reshape(width, 3, local)
    params = (norms[:2], norms[2:], wqkv, wout, wup, wdown)

    received = None
    runs = []
    for tick in range(micro + 1):
        own = inputs[min(tick, micro - 1)]
        entering = own if received is None else jnp.where(lead, own, received)
        result, saved = layer_forward(entering, params)
        runs.append((result,) + saved)
        if tick < micro:
            received = shifted(result, "section", 1)
    store = [
        tuple(jnp.where(lead, a, b) for a, b in zip(runs[m], runs[m + 1])) for m in range(micro)
    ]

    incoming = None
    backs = []
    for tick in range(micro + 1):
        early, late = max(tick - 1, 0), min(tick, micro - 1)
        record = store[early]
        grad = cotangent[0, early]
        if early != late:
            record = tuple(jnp.where(lead, a, b) for a, b in zip(record, store[late]))
            grad = jnp.where(lead, grad, cotangent[0, late])
        if incoming is not None:
            grad = grad + jnp.where(lead, incoming, 0.0)
        held = ()
        if tick == micro:
            halves = [item[1] for item in backs] + [grad.astype(jnp.bfloat16)]
            halves = [jnp.where(lead, halves[m + 1], halves[m]) for m in range(micro)]
            right = jnp.concatenate(halves)
            down = scatter_begin(over_tokens(store, 11, right), 1)
            held = down[1]
        back, held = layer_backward(grad, record[1:], params, held)
        backs.append(back)
        if tick < micro:
            incoming = shifted(back[0], "section", -1)
    done = [
        tuple(jnp.where(lead, a, b) for a, b in zip(backs[m + 1], backs[m])) for m in range(micro)
    ]

    down = (down[0], held)
    up = scatter_begin(over_tokens(store, 4, jnp.concatenate([d[2] for d in done])), 0, down[1])
    qkv = scatter_begin(over_tokens(store, 3, jnp.concatenate([d[3] for d in done])), 0, up[1])
    out = scatter_begin(over_tokens(store, 8, right), 1, qkv[1])
    d_norms = sum(item[4] for item in done)
    d_norms = d_norms + lax.ppermute(d_norms, "tensor", [(0, 1), (1, 0)])
    d_norms = scatter_end(scatter_begin(d_norms, 1, (), jnp.float32), 1, jnp.float32)
    down_grads = scatter_end(down, 1)
    up_grads = scatter_end(up, 0)
    qkv_grads = scatter_end(qkv, 0).reshape(-1, 3, local)
    out_grads = scatter_end(out, 1)
    return (
        jnp.stack([item[0] for item in store])[None],
        jnp.stack([item[0] for item in done])[None],
        d_norms[None, :2],
        d_norms[None, 2:],
        qkv_grads[None],
        out_grads[None],
        up_grads[None],
        down_grads[None],
    )


def solution(mesh):
    in_specs = (
        P(None, "fsdp", None),
        P("section", None, "fsdp", None),
        P("section", None, "fsdp"),
        P("section", None, "fsdp"),
        P("section", "fsdp", None, "tensor"),
        P("section", "tensor", "fsdp"),
        P("section", "fsdp", "tensor"),
        P("section", "tensor", "fsdp"),
    )
    out_specs = (
        P("section", None, "fsdp", None),
        P("section", None, "fsdp", None),
        P("section", None, "fsdp"),
        P("section", None, "fsdp"),
        P("section", "fsdp", None, "tensor"),
        P("section", "tensor", "fsdp"),
        P("section", "fsdp", "tensor"),
        P("section", "tensor", "fsdp"),
    )
    return jax.shard_map(shards, mesh=mesh, in_specs=in_specs, out_specs=out_specs, check_vma=False)
```

```python
import math

import jax
import jax.numpy as jnp
from jax import lax
from jax.sharding import PartitionSpec as P

HD = 64
SEQ = 128


EPS = 1e-05


def shifted(x, axis, by):
    peers = lax.axis_size(axis)
    pairs = [(i, i + by) for i in range(peers) if 0 <= i + by < peers]
    return lax.ppermute(x, axis, pairs)


def swap_sum(x, axis):
    half = x.astype(jnp.bfloat16)
    other = lax.ppermute(half, axis, [(0, 1), (1, 0)])
    return half.astype(jnp.float32) + other.astype(jnp.float32)


def pair_sum(x, axis):
    if lax.axis_size(axis) == 2:
        return swap_sum(x, axis)
    return lax.psum(x, axis)


def turned(peers, by):
    return [(i, (i + 2 * by) % peers) for i in range(peers)]


def crossed(peers):
    return [(i, i ^ 1) for i in range(peers)]


def gather(x, axis, after=()):
    peers = lax.axis_size("fsdp")
    if peers != 8:
        return (lax.all_gather(x, "fsdp", axis=axis, tiled=True), ())
    lines = peers // 2
    me = lax.axis_index("fsdp")
    line, side = me // 2, me % 2
    width = x.shape[axis]
    shape = x.shape[:axis] + (peers * width,) + x.shape[axis + 1 :]
    whole = jnp.zeros(shape, x.dtype)
    start = x
    if after:
        start, after = lax.optimization_barrier((x, after))
    own = [x] + [lax.ppermute(start, "fsdp", turned(peers, by)) for by in range(1, lines)]
    for by, block in enumerate(own):
        other = lax.ppermute(block, "fsdp", crossed(peers))
        source = 2 * ((line - by) % lines)
        whole = lax.dynamic_update_slice_in_dim(whole, block, (source + side) * width, axis)
        whole = lax.dynamic_update_slice_in_dim(whole, other, (source + 1 - side) * width, axis)
    return (whole, tuple(own[1:2]))


TURNS = (2, 1, 3, 0)


def scatter_begin(x, axis, after=(), sent=jnp.bfloat16):
    peers = lax.axis_size("fsdp")
    if peers != 8:
        return (x, ())
    lines = peers // 2
    me = lax.axis_index("fsdp")
    line, side = me // 2, me % 2
    width = x.shape[axis] // peers

    def block(by, side):
        place = 2 * ((line + by) % lines) + side
        return lax.dynamic_slice_in_dim(x, place * width, width, axis)

    away = tuple(block(by, 1 - side).astype(sent) for by in TURNS)
    if after:
        away, after = lax.optimization_barrier((away, after))
    came = tuple(lax.ppermute(item, "fsdp", crossed(peers)) for item in away)
    return (tuple(block(by, side) for by in TURNS), came)


def scatter_end(begun, axis, sent=jnp.bfloat16):
    mine, came = begun
    peers = lax.axis_size("fsdp")
    if peers != 8:
        return lax.psum_scatter(
            mine.astype(sent), "fsdp", scatter_dimension=axis, tiled=True
        ).astype(jnp.float32)
    total = None
    for by, left, right in zip(TURNS, mine, came):
        part = left + right.astype(jnp.float32)
        if by:
            part = lax.ppermute(part.astype(sent), "fsdp", turned(peers, by)).astype(jnp.float32)
        total = part if total is None else total + part
    return total


def angles(positions, head_dim):
    rot = head_dim // 4
    half = rot // 2
    freq = 10000.0 ** (-(jnp.arange(half).astype(jnp.float32) * 2.0 / rot))
    theta = positions.astype(jnp.float32)[:, None] * freq[None, :]
    return (jnp.cos(theta), jnp.sin(theta))


def rotate(value, cosine, sine):
    half = cosine.shape[1]
    first = value[..., :half]
    second = value[..., half : 2 * half]
    rest = value[..., 2 * half :]
    cpart = cosine[:, None, :]
    spart = sine[:, None, :]
    return jnp.concatenate(
        [first * cpart - second * spart, second * cpart + first * spart, rest], axis=-1
    )


def normalize(u):
    whole = u.astype(jnp.float32)
    centred = whole - jnp.mean(whole, axis=-1, keepdims=True)
    rstd = lax.rsqrt(jnp.mean(centred * centred, axis=-1, keepdims=True) + EPS)
    return (centred * rstd, rstd)


def gelu_slope(hidden):
    return 0.5 * (1.0 + lax.erf(hidden / math.sqrt(2.0))) + hidden * jnp.exp(
        -0.5 * hidden * hidden
    ) / math.sqrt(2.0 * math.pi)


def grouped(value):
    return value.reshape((value.shape[0] // SEQ, SEQ) + value.shape[1:])


def masked_scores(query, key):
    scores = jnp.einsum("sqhd,skhd->shqk", query, key, preferred_element_type=jnp.float32)
    places = jnp.arange(SEQ, dtype=jnp.int32)
    return jnp.where(places[None, :] <= places[:, None], scores, -1e30)


def attention_forward(query, key, value):
    tokens, heads = (query.shape[0], query.shape[1])
    scores = masked_scores(grouped(query), grouped(key))
    top = jnp.max(scores, axis=-1, keepdims=True)
    lse = top + jnp.log(jnp.sum(jnp.exp(scores - top), axis=-1, keepdims=True))
    probs = jnp.exp(scores - lse).astype(jnp.bfloat16)
    attended = jnp.einsum(
        "shqk,skhd->sqhd", probs, grouped(value), preferred_element_type=jnp.float32
    )
    return (attended.reshape(tokens, heads, HD), lse[..., 0])


def attention_backward(query, key, value, lse, d_att, attended):
    tokens, heads = (query.shape[0], query.shape[1])
    delta = jnp.sum(d_att.astype(jnp.float32) * attended.astype(jnp.float32), axis=-1)
    delta = jnp.swapaxes(grouped(delta), 1, 2)
    query_s, key_s, value_s, grads_s = (
        grouped(query),
        grouped(key),
        grouped(value),
        grouped(d_att),
    )
    probs = jnp.exp(masked_scores(query_s, key_s) - lse[..., None])
    d_probs = jnp.einsum("sqhd,skhd->shqk", grads_s, value_s, preferred_element_type=jnp.float32)
    d_scores = (probs * (d_probs - delta[..., None])).astype(jnp.bfloat16)
    d_query = jnp.einsum("shqk,skhd->sqhd", d_scores, key_s, preferred_element_type=jnp.float32)
    d_key = jnp.einsum("shqk,sqhd->skhd", d_scores, query_s, preferred_element_type=jnp.float32)
    d_value = jnp.einsum(
        "shqk,sqhd->skhd", probs.astype(jnp.bfloat16), grads_s, preferred_element_type=jnp.float32
    )
    shape = (tokens, heads, HD)
    return (d_query.reshape(shape), d_key.reshape(shape), d_value.reshape(shape))


def layer_forward(u, params):
    gains, biases, wqkv, wout, wup, wdown = params
    tokens, width = u.shape
    local = wqkv.shape[2]
    heads = local // HD
    normed, rstd = normalize(u)
    gain = gains.astype(jnp.float32)
    bias = biases.astype(jnp.float32)
    first = (normed * gain[0] + bias[0]).astype(jnp.bfloat16)
    second = (normed * gain[1] + bias[1]).astype(jnp.bfloat16)
    qkv = jnp.dot(
        first, wqkv.reshape(width, 3 * local), preferred_element_type=jnp.float32
    ).reshape(tokens, 3, heads, HD)
    qpos = jnp.arange(tokens, dtype=jnp.int32) % SEQ
    cosine, sine = angles(qpos, HD)
    query = (rotate(qkv[:, 0], cosine, sine) * HD ** (-0.5)).astype(jnp.bfloat16)
    key = rotate(qkv[:, 1], cosine, sine).astype(jnp.bfloat16)
    value = qkv[:, 2].astype(jnp.bfloat16)
    attended, lse = attention_forward(query, key, value)
    attended = attended.astype(jnp.bfloat16).reshape(tokens, local)
    hidden = jnp.dot(second, wup, preferred_element_type=jnp.float32)
    act = jax.nn.gelu(hidden, approximate=False).astype(jnp.bfloat16)
    branch = jnp.dot(attended, wout, preferred_element_type=jnp.float32) + jnp.dot(
        act, wdown, preferred_element_type=jnp.float32
    )
    total = pair_sum(branch, "tensor")
    result = (u.astype(jnp.float32) + total).astype(jnp.bfloat16)
    return (result, (normed, rstd, first, second, query, key, value, attended, lse, hidden, act))


def layer_backward(grad, saved, params, held=()):
    normed, rstd, first, second, query, key, value, attended, lse, hidden, act = saved
    gains, biases, wqkv, wout, wup, wdown = params
    tokens, width = grad.shape
    local = wqkv.shape[2]
    heads = local // HD
    grad_half = grad.astype(jnp.bfloat16)
    d_act = jnp.dot(grad_half, wdown.T, preferred_element_type=jnp.float32)
    d_hidden = (d_act * gelu_slope(hidden)).astype(jnp.bfloat16)
    d_second = jnp.dot(d_hidden, wup.T, preferred_element_type=jnp.float32)
    d_att = (
        jnp.dot(grad_half, wout.T, preferred_element_type=jnp.float32)
        .astype(jnp.bfloat16)
        .reshape(tokens, heads, HD)
    )
    d_query, d_key, d_value = attention_backward(
        query, key, value, lse, d_att, attended.reshape(tokens, heads, HD)
    )
    qpos = jnp.arange(tokens, dtype=jnp.int32) % SEQ
    cosine, sine = angles(qpos, HD)
    dq_back = rotate(d_query * HD ** (-0.5), cosine, -sine)
    dk_back = rotate(d_key, cosine, -sine)
    d_qkv = (
        jnp.stack([dq_back, dk_back, d_value], axis=1)
        .astype(jnp.bfloat16)
        .reshape(tokens, 3 * local)
    )
    d_first = jnp.dot(d_qkv, wqkv.reshape(width, 3 * local).T, preferred_element_type=jnp.float32)
    gain = gains.astype(jnp.float32)
    d_norms = jnp.stack(
        [
            jnp.sum(d_first * normed, axis=0),
            jnp.sum(d_second * normed, axis=0),
            jnp.sum(d_first, axis=0),
            jnp.sum(d_second, axis=0),
        ]
    )
    d_norm = d_first * gain[0] + d_second * gain[1]
    if held:
        d_norm, held = lax.optimization_barrier((d_norm, held))
    d_norm = pair_sum(d_norm, "tensor")
    d_input = grad + rstd * (
        d_norm
        - jnp.mean(d_norm, axis=-1, keepdims=True)
        - normed * jnp.mean(d_norm * normed, axis=-1, keepdims=True)
    )
    return ((d_input, grad_half, d_hidden, d_qkv, d_norms), held)


def over_tokens(store, place, right):
    left = jnp.concatenate([item[place] for item in store])
    return jnp.dot(left.T, right, preferred_element_type=jnp.float32)


def shards(inputs, cotangent, norm_gains, norm_biases, w_qkv, w_out, w_up, w_down):
    section = lax.axis_index("section")
    lead = section == 0
    micro = inputs.shape[0]
    width = inputs.shape[2]
    local = w_qkv.shape[3]
    norms, _ = gather(jnp.concatenate([norm_gains[0], norm_biases[0]]), 1)
    wqkv, after = gather(w_qkv[0].reshape(-1, 3 * local), 0)
    wup, after = gather(w_up[0], 0, after)
    wdown, after = gather(w_down[0], 1, after)
    wout, after = gather(w_out[0], 1, after)
    wqkv = wqkv.reshape(width, 3, local)
    params = (norms[:2], norms[2:], wqkv, wout, wup, wdown)

    received = None
    runs = []
    for tick in range(micro + 1):
        own = inputs[min(tick, micro - 1)]
        entering = own if received is None else jnp.where(lead, own, received)
        result, saved = layer_forward(entering, params)
        runs.append((result,) + saved)
        if tick < micro:
            received = shifted(result, "section", 1)
    store = [
        tuple(jnp.where(lead, a, b) for a, b in zip(runs[m], runs[m + 1])) for m in range(micro)
    ]

    incoming = None
    backs = []
    for tick in range(micro + 1):
        early, late = max(tick - 1, 0), min(tick, micro - 1)
        record = store[early]
        grad = cotangent[0, early]
        if early != late:
            record = tuple(jnp.where(lead, a, b) for a, b in zip(record, store[late]))
            grad = jnp.where(lead, grad, cotangent[0, late])
        if incoming is not None:
            grad = grad + jnp.where(lead, incoming, 0.0)
        held = ()
        if tick == micro:
            halves = [item[1] for item in backs] + [grad.astype(jnp.bfloat16)]
            halves = [jnp.where(lead, halves[m + 1], halves[m]) for m in range(micro)]
            right = jnp.concatenate(halves)
            down = scatter_begin(over_tokens(store, 11, right), 1)
            held = down[1][:2]
        back, held = layer_backward(grad, record[1:], params, held)
        backs.append(back)
        if tick < micro:
            incoming = shifted(back[0], "section", -1)
    done = [
        tuple(jnp.where(lead, a, b) for a, b in zip(backs[m + 1], backs[m])) for m in range(micro)
    ]

    down = (down[0], held + down[1][2:])
    up = scatter_begin(over_tokens(store, 4, jnp.concatenate([d[2] for d in done])), 0, down[1][:2])
    qkv = scatter_begin(over_tokens(store, 3, jnp.concatenate([d[3] for d in done])), 0, up[1][:2])
    out = scatter_begin(over_tokens(store, 8, right), 1, qkv[1][:2])
    d_norms = sum(item[4] for item in done)
    d_norms = d_norms + lax.ppermute(d_norms, "tensor", [(0, 1), (1, 0)])
    d_norms = scatter_end(scatter_begin(d_norms, 1, qkv[1][:2], jnp.float32), 1, jnp.float32)
    down_grads = scatter_end(down, 1)
    up_grads = scatter_end(up, 0)
    qkv_grads = scatter_end(qkv, 0).reshape(-1, 3, local)
    out_grads = scatter_end(out, 1)
    return (
        jnp.stack([item[0] for item in store])[None],
        jnp.stack([item[0] for item in done])[None],
        d_norms[None, :2],
        d_norms[None, 2:],
        qkv_grads[None],
        out_grads[None],
        up_grads[None],
        down_grads[None],
    )


def solution(mesh):
    in_specs = (
        P(None, "fsdp", None),
        P("section", None, "fsdp", None),
        P("section", None, "fsdp"),
        P("section", None, "fsdp"),
        P("section", "fsdp", None, "tensor"),
        P("section", "tensor", "fsdp"),
        P("section", "fsdp", "tensor"),
        P("section", "tensor", "fsdp"),
    )
    out_specs = (
        P("section", None, "fsdp", None),
        P("section", None, "fsdp", None),
        P("section", None, "fsdp"),
        P("section", None, "fsdp"),
        P("section", "fsdp", None, "tensor"),
        P("section", "tensor", "fsdp"),
        P("section", "fsdp", "tensor"),
        P("section", "tensor", "fsdp"),
    )
    return jax.shard_map(shards, mesh=mesh, in_specs=in_specs, out_specs=out_specs, check_vma=False)
```
